32 devices in a mesh: mode: 8 (over z, y), space: 4 (over x, core).
Axes of the slice: x: 2, y: 2, z: 4, core: 2. Of those that a mesh axis runs over, the one named last changes fastest.
Arguments:
- modes: bfloat16 [3, 256, 16, 4, 128], P(None, 'mode', 'space'), may hold values from -6 to 6
- weights: float32 [16, 4, 128], P('space'), may hold values from 0.001275776 to 0.031894397
- plan: int32 [3], replicated, may hold values from 0 to 7, as said below
Outputs:
- convection: float32 [128, 32, 256], P('space', None, 'mode')
The draws below stay inside these ranges and needn't reach their ends.
Inputs may be any that keep to these rules, and one draw needn't show every extreme that they name: plan[0] is 256 / 32 - 1, the last aligned block of 32 modes; plan[1] to plan[2] are distinct indices of aligned panels of 64 modes, below 256 / 64.
All inputs are finite; a program needn't handle non-finite values.
Results may differ from the reference program's by a relative error of at most 0.0041.
Values may be sent and summed in bfloat16 or wider, within the bound.
A program may use at most 128 MiB of HBM per device.

```python
import math
import jax
import jax.numpy as jnp
from jax import lax

M_DEV = 32
MODES = 256
PANEL = 64
NPANEL = 2
TESTS = 128
CY = 4
CZ = 128
NX = 16


def draw_plan(key, part):
    panel_key = jax.random.fold_in(key, 23)
    owner = jnp.full((1,), MODES // M_DEV - 1, dtype=jnp.int32)
    panels = jax.random.permutation(panel_key, jnp.arange(MODES // PANEL, dtype=jnp.int32))[:NPANEL]
    return jnp.concatenate([owner, panels.astype(jnp.int32)]).astype(jnp.int32)


def block_levels(own_key, dims, shards, least, high):
    loudness = 1.0
    for dim, shards_of in shards:
        steps = jax.random.uniform(jax.random.fold_in(jax.random.fold_in(own_key, 6), dim), (shards_of,), jnp.float32, least / len(shards), high / len(shards))
        loudness = loudness * jnp.repeat(jnp.exp(steps), dims[dim] // shards_of).reshape((-1,) + (1,) * (len(dims) - 1 - dim))
    return loudness


def noise(key, shape, width, most, cuts=(), held_as=jnp.bfloat16):
    array = width * jax.random.normal(key, shape, jnp.float32)
    if cuts:
        array = array * block_levels(key, shape, cuts, -0.22, 0.18)
    return jnp.clip(array, -most, most).astype(held_as)


def setup_inputs(seed: int = 0) -> dict:
    arg_keys = jax.random.split(jax.random.key(seed), 4)
    return {
        "modes": noise(arg_keys[0], (3, MODES, NX, CY, CZ), 1.0, 6.0, ((1, 8), (2, 4))),
        "weights": jnp.clip(jnp.exp(math.log(0.031894397) - 3.218876 * jax.random.uniform(arg_keys[1], (NX, CY, CZ), jnp.float32) ** block_levels(arg_keys[1], (NX, CY, CZ), ((0, 4),), -0.2, 0.2)), 0.001275776, 0.031894397),
        "plan": draw_plan(jax.random.fold_in(arg_keys[3], 71), 0),
    }


def reference(modes, weights, plan):
    advecting = lax.dynamic_slice_in_dim(modes, (plan[0] * M_DEV).astype(jnp.int32), M_DEV, 1)
    panels = [lax.dynamic_slice_in_dim(modes, (plan[1 + panel] * PANEL).astype(jnp.int32), PANEL, 1) for panel in range(NPANEL)]
    tests = jnp.concatenate(panels, axis=1)
    weighted = (weights[None, None] * tests.astype(jnp.float32)).astype(jnp.bfloat16)

    def plane_step(total, plane):
        before = jnp.mod(plane - 1, NX).astype(jnp.int32)
        after = jnp.mod(plane + 1, NX).astype(jnp.int32)
        center = lax.dynamic_index_in_dim(modes, plane, 2, keepdims=False).astype(jnp.float32)
        lower = lax.dynamic_index_in_dim(modes, before, 2, keepdims=False).astype(jnp.float32)
        upper = lax.dynamic_index_in_dim(modes, after, 2, keepdims=False).astype(jnp.float32)
        grad_x = 0.5 * (upper - lower)
        grad_y = 0.5 * (jnp.roll(center, -1, axis=2) - jnp.roll(center, 1, axis=2))
        grad_z = 0.5 * (jnp.roll(center, -1, axis=3) - jnp.roll(center, 1, axis=3))
        advect = lax.dynamic_index_in_dim(advecting, plane, 2, keepdims=False).astype(jnp.float32)
        values = advect[0][None, :, None] * grad_x[:, None]
        values = values + advect[1][None, :, None] * grad_y[:, None]
        values = values + advect[2][None, :, None] * grad_z[:, None]
        values = values.astype(jnp.bfloat16).reshape(3, M_DEV * MODES, CY * CZ)
        tested = lax.dynamic_index_in_dim(weighted, plane, 2, keepdims=False).reshape(3, TESTS, CY * CZ)
        total = total + lax.dot_general(tested, values, (((0, 2), (0, 2)), ((), ())), preferred_element_type=jnp.float32)
        return total, None

    start_total = jnp.zeros((TESTS, M_DEV * MODES), jnp.float32)
    total, unused = lax.scan(plane_step, start_total, jnp.arange(NX, dtype=jnp.int32))
    return total.reshape(TESTS, M_DEV, MODES)
```

```python
import functools

import jax
import jax.numpy as jnp
from jax import lax
from jax.experimental import pallas as pl
from jax.experimental.pallas import tpu as pltpu
from jax.sharding import PartitionSpec as P

PANEL = 64
NPANEL = 2
MESH = pl.DeviceIdType.MESH
F32 = jnp.float32
BF16 = jnp.bfloat16


def kernel(dims, plan_ref, modes_ref, weights_ref, out_ref,
           ext, advb, up_in, dn_in, up_out, dn_out, tests, advf, vals, wts, acc, tot, stage, rs_in,
           halo_send, halo_recv, up_send, up_recv, dn_send, dn_recv, y_send, y_recv,
           ad_send, ay_send, adv_recv, rs_send, rs_recv):
    panels, spaces, cy, own_rows = dims
    comps, cells, nm, lanes = modes_ref.shape
    halves = 2
    hc = cells // halves
    chunks = comps * NPANEL * halves
    pairs = cells // 2
    quarter = pairs // 2
    last = panels - 1
    mode = lax.axis_index("mode")
    p = mode // 2
    q = lax.rem(mode, 2)
    me = lax.axis_index("space")
    partner = p * 2 + (1 - q)
    below = lax.rem(p + panels - 1, panels) * 2 + q
    above = lax.rem(p + 1, panels) * 2 + q
    right = lax.rem(me + 1, spaces)
    left = lax.rem(me + spaces - 1, spaces)
    is_src = jnp.logical_and(p == last, q == 1)
    not_src = jnp.logical_or(p < last, q == 0)

    barrier = pltpu.get_barrier_semaphore()
    for other in (partner, below, above):
        pl.semaphore_signal(barrier, inc=1, device_id={"mode": other}, device_id_type=MESH)
    for d in range(1, spaces):
        pl.semaphore_signal(barrier, inc=1, device_id={"space": lax.rem(me + d, spaces)}, device_id_type=MESH)

    def chunk_of(m):
        c = m // (NPANEL * halves)
        t = lax.rem(m // halves, NPANEL)
        h = lax.rem(m, halves)
        return c, t, h

    ext[:, cy : cy + cells] = modes_ref[...]

    @pl.when(is_src)
    def _():
        for a in range(pairs):
            advb[a] = modes_ref[:, 2 * a : 2 * a + 2]

    @pl.when(p == 0)
    def _():
        for m in range(chunks):
            c, t, h = m // (NPANEL * halves), (m // halves) % NPANEL, m % halves
            up_in[m] = modes_ref[c, h * hc : (h + 1) * hc]

    @pl.when(p == last)
    def _():
        for m in range(chunks):
            c, t, h = m // (NPANEL * halves), (m // halves) % NPANEL, m % halves
            dn_in[m] = modes_ref[c, h * hc : (h + 1) * hc]

    pl.semaphore_wait(barrier, 3 + spaces - 1)

    def copy_adv_down(a):
        return pltpu.make_async_remote_copy(
            src_ref=advb.at[q * quarter + a], dst_ref=advb.at[q * quarter + a],
            send_sem=ad_send.at[a], recv_sem=adv_recv.at[q * quarter + a],
            device_id={"mode": below}, device_id_type=MESH)

    def copy_adv_side(x):
        return pltpu.make_async_remote_copy(
            src_ref=advb.at[x], dst_ref=advb.at[x],
            send_sem=ay_send.at[x], recv_sem=adv_recv.at[x],
            device_id={"mode": partner}, device_id_type=MESH)

    def copy_up(m):
        return pltpu.make_async_remote_copy(
            src_ref=up_out.at[m], dst_ref=up_in.at[m], send_sem=up_send.at[m], recv_sem=up_recv.at[m],
            device_id={"mode": above}, device_id_type=MESH)

    def copy_down(m):
        return pltpu.make_async_remote_copy(
            src_ref=dn_out.at[m], dst_ref=dn_in.at[m], send_sem=dn_send.at[m], recv_sem=dn_recv.at[m],
            device_id={"mode": below}, device_id_type=MESH)

    def copy_side(m):
        return pltpu.make_async_remote_copy(
            src_ref=tests.at[m, q], dst_ref=tests.at[m, q], send_sem=y_send.at[m], recv_sem=y_recv.at[m],
            device_id={"mode": partner}, device_id_type=MESH)

    @pl.when(is_src)
    def _():
        for a in range(pairs):
            copy_adv_side(a).start()

    halo_up = pltpu.make_async_remote_copy(
        src_ref=modes_ref.at[:, pl.ds(cells - cy, cy)], dst_ref=ext.at[:, pl.ds(0, cy)],
        send_sem=halo_send.at[0], recv_sem=halo_recv.at[0], device_id={"space": right}, device_id_type=MESH)
    halo_down = pltpu.make_async_remote_copy(
        src_ref=modes_ref.at[:, pl.ds(0, cy)], dst_ref=ext.at[:, pl.ds(cells + cy, cy)],
        send_sem=halo_send.at[1], recv_sem=halo_recv.at[1], device_id={"space": left}, device_id_type=MESH)
    halo_up.start()
    halo_down.start()

    def values_of(xp):
        adv_at = advb.at[xp]
        for e in range(2):
            xy = 2 * xp + e
            x = xy // cy
            y = lax.rem(xy, cy)
            y_next = cy + x * cy + lax.rem(y + 1, cy)
            y_prev = cy + x * cy + lax.rem(y + cy - 1, cy)
            for d in range(3):
                advf[e, d] = adv_at[d, e].astype(F32)
            grads = []
            for c in range(comps):
                center = ext[c, xy + cy].astype(F32)
                gx = 0.5 * (ext[c, xy + 2 * cy].astype(F32) - ext[c, xy].astype(F32))
                gy = 0.5 * (ext[c, y_next].astype(F32) - ext[c, y_prev].astype(F32))
                gz = 0.5 * (pltpu.roll(center, lanes - 1, 1) - pltpu.roll(center, 1, 1))
                grads.append((gx, gy, gz))

            def row(j, carry):
                rows = [jnp.broadcast_to(advf[e, d, pl.ds(j, 1), :], (nm, lanes)) for d in range(3)]
                for c in range(comps):
                    value = rows[0] * grads[c][0] + rows[1] * grads[c][1] + rows[2] * grads[c][2]
                    start = pl.multiple_of(j * nm, nm)
                    vals[c * pairs + xp, pl.ds(start, nm), e * lanes : (e + 1) * lanes] = value.astype(BF16)
                return carry

            lax.fori_loop(0, nm, row, 0, unroll=4)

    ticks = chunks + quarter + last + 1

    def tick(step, carry):
        a = step - (last - p)

        @pl.when(jnp.logical_and(a >= 0, a < quarter))
        def _():
            @pl.when(not_src)
            def _():
                copy_adv_side(q * quarter + a).wait_recv()

            @pl.when(p > 0)
            def _():
                copy_adv_down(a).start()

            @pl.when(p < last)
            def _():
                copy_adv_side(q * quarter + a).start()

        mu = step - p

        @pl.when(jnp.logical_and(mu >= 0, mu < chunks))
        def _():
            @pl.when(p > 0)
            def _():
                copy_up(mu).wait_recv()

            @pl.when(p < last)
            def _():
                c, t, h = chunk_of(mu)
                mine = modes_ref[c, pl.ds(h * hc, hc)]
                up_out[mu] = jnp.where(plan_ref[1 + t] == p, mine, up_in[mu])
                copy_up(mu).start()

        md = step - quarter - (last - p)

        @pl.when(jnp.logical_and(md >= 0, md < chunks))
        def _():
            @pl.when(p < last)
            def _():
                copy_down(md).wait_recv()

            @pl.when(p > 0)
            def _():
                c, t, h = chunk_of(md)
                mine = modes_ref[c, pl.ds(h * hc, hc)]
                dn_out[md] = jnp.where(plan_ref[1 + t] == p, mine, dn_in[md])
                copy_down(md).start()

        mf = step - jnp.maximum(p, quarter + last - p)

        @pl.when(jnp.logical_and(mf >= 0, mf < chunks))
        def _():
            c, t, h = chunk_of(mf)
            mine = modes_ref[c, pl.ds(h * hc, hc)]
            owner = plan_ref[1 + t]
            got = jnp.where(owner < p, up_in[mf], dn_in[mf])
            tests[mf, q] = jnp.where(owner == p, mine, got)
            copy_side(mf).start()

        return carry

    lax.fori_loop(0, ticks, tick, 0)

    halo_up.wait_recv()
    halo_down.wait_recv()

    @pl.when(not_src)
    def _():
        def take(a, carry):
            copy_adv_side((1 - q) * quarter + a).wait_recv()
            return carry
        lax.fori_loop(0, quarter, take, 0)

    def values_step(xp, carry):
        values_of(xp)
        return carry

    lax.fori_loop(0, pairs, values_step, 0)

    def take_side(m, carry):
        copy_side(m).wait_recv()
        return carry

    lax.fori_loop(0, chunks, take_side, 0)
    acc[...] = jnp.zeros_like(acc)

    def gemm(kb, carry):
        c = kb // pairs
        xp = lax.rem(kb, pairs)
        for e in range(2):
            xy = 2 * xp + e
            h = xy // hc
            xl = lax.rem(xy, hc)
            weight = weights_ref[pl.ds(xy, 1), :]
            for t in range(NPANEL):
                for s in range(2):
                    raw = tests[(c * NPANEL + t) * halves + h, s, xl].astype(F32)
                    r = (t * 2 + s) * nm
                    wts[r : r + nm, e * lanes : (e + 1) * lanes] = (weight * raw).astype(BF16)
        acc[...] += lax.dot_general(vals[kb], wts[...], (((1,), (1,)), ((), ())), preferred_element_type=F32)
        return carry

    lax.fori_loop(0, comps * pairs, gemm, 0)

    for jt in range(nm * nm // lanes):
        turned = acc[jt * lanes : (jt + 1) * lanes, :].T
        for s in range(spaces):
            piece = turned[s * own_rows : (s + 1) * own_rows]
            tot[s, :, jt * lanes : (jt + 1) * lanes] = piece
            stage[s, :, jt * lanes : (jt + 1) * lanes] = piece.astype(BF16)

    copies = []
    for d in range(1, spaces):
        peer = lax.rem(me + d, spaces)
        copies.append(pltpu.make_async_remote_copy(
            src_ref=stage.at[peer], dst_ref=rs_in.at[d - 1], send_sem=rs_send.at[d - 1],
            recv_sem=rs_recv.at[d - 1], device_id={"space": peer}, device_id_type=MESH))
    for copy in copies:
        copy.start()

    halo_up.wait_send()
    halo_down.wait_send()

    @pl.when(is_src)
    def _():
        for a in range(pairs):
            copy_adv_side(a).wait_send()

    @pl.when(p < last)
    def _():
        def done(a, carry):
            copy_adv_side(q * quarter + a).wait_send()
            return carry
        lax.fori_loop(0, quarter, done, 0)

        def done_up(m, carry):
            copy_up(m).wait_send()
            return carry
        lax.fori_loop(0, chunks, done_up, 0)

    @pl.when(p > 0)
    def _():
        def done(a, carry):
            copy_adv_down(a).wait_send()
            return carry
        lax.fori_loop(0, quarter, done, 0)

        def done_down(m, carry):
            copy_down(m).wait_send()
            return carry
        lax.fori_loop(0, chunks, done_down, 0)

    def done_side(m, carry):
        copy_side(m).wait_send()
        return carry

    lax.fori_loop(0, chunks, done_side, 0)

    total = tot[me]
    for d, copy in enumerate(copies):
        copy.wait_recv()
        total = total + rs_in[d].astype(F32)
    out_ref[...] = total
    for copy in copies:
        copy.wait_send()


def solution(mesh):
    nmode, spaces = mesh.shape["mode"], mesh.shape["space"]

    def local(modes, weights, plan):
        comps, nm, nx, cy, lanes = modes.shape
        cells = nx * cy
        assert PANEL == 2 * nm and nmode % 2 == 0
        test_count = NPANEL * PANEL
        own_rows = test_count // spaces
        turned = modes.transpose(0, 2, 3, 1, 4).reshape(comps, cells, nm, lanes)
        hc, pairs = cells // 2, cells // 2
        chunks = comps * NPANEL * 2
        quarter = pairs // 2
        vm = pl.BlockSpec(memory_space=pltpu.VMEM)
        chunk = (chunks, hc, nm, lanes)
        dma = pltpu.SemaphoreType.DMA
        out = pl.pallas_call(
            functools.partial(kernel, (nmode // 2, spaces, cy, own_rows)),
            out_shape=jax.ShapeDtypeStruct((own_rows, nm * nm), F32),
            in_specs=[pl.BlockSpec(memory_space=pltpu.SMEM), vm, vm],
            out_specs=vm,
            scratch_shapes=[
                pltpu.VMEM((comps, cells + 2 * cy, nm, lanes), BF16),
                pltpu.VMEM((pairs, comps, 2, nm, lanes), BF16),
                pltpu.VMEM(chunk, BF16), pltpu.VMEM(chunk, BF16), pltpu.VMEM(chunk, BF16), pltpu.VMEM(chunk, BF16),
                pltpu.VMEM((chunks, 2, hc, nm, lanes), BF16),
                pltpu.VMEM((2, comps, nm, lanes), F32),
                pltpu.VMEM((comps * pairs, nm * nm, 2 * lanes), BF16),
                pltpu.VMEM((test_count, 2 * lanes), BF16),
                pltpu.VMEM((nm * nm, test_count), F32),
                pltpu.VMEM((spaces, own_rows, nm * nm), F32),
                pltpu.VMEM((spaces, own_rows, nm * nm), BF16),
                pltpu.VMEM((spaces - 1, own_rows, nm * nm), BF16),
                dma((2,)), dma((2,)),
                dma((chunks,)), dma((chunks,)), dma((chunks,)), dma((chunks,)), dma((chunks,)), dma((chunks,)),
                dma((quarter,)), dma((pairs,)), dma((pairs,)),
                dma((spaces - 1,)), dma((spaces - 1,)),
            ],
            compiler_params=pltpu.CompilerParams(
                collective_id=0, has_side_effects=True, vmem_limit_bytes=48 * 1024 * 1024),
        )(plan, turned, weights.reshape(cells, lanes))
        return out.reshape(own_rows, nm, nm)

    in_specs = (P(None, "mode", "space", None, None), P("space", None, None), P())
    return jax.shard_map(local, mesh=mesh, in_specs=in_specs, out_specs=P("space", None, "mode"), check_vma=False)
```

```python
import functools

import jax
import jax.numpy as jnp
from jax import lax
from jax.experimental import pallas as pl
from jax.experimental.pallas import tpu as pltpu
from jax.sharding import PartitionSpec as P

PANEL = 64
NPANEL = 2
SKEW = 3
MESH = pl.DeviceIdType.MESH
F32 = jnp.float32
BF16 = jnp.bfloat16


def kernel(dims, plan_ref, modes_ref, weights_ref, out_ref,
           ext, advb, up_in, dn_in, up_out, dn_out, tests, advf, vals, wts, acc, tot, stage, rs_in,
           halo_send, halo_recv, up_send, up_recv, dn_send, dn_recv, y_send, y_recv,
           ad_send, ay_send, adv_recv, rs_send, rs_recv):
    panels, spaces, cy, own_rows = dims
    comps, cells, nm, lanes = modes_ref.shape
    halves = 2
    hc = cells // halves
    chunks = comps * NPANEL * halves
    pairs = cells // 2
    quarter = pairs // 2
    last = panels - 1
    mode = lax.axis_index("mode")
    p = mode // 2
    q = lax.rem(mode, 2)
    me = lax.axis_index("space")
    partner = p * 2 + (1 - q)
    below = lax.rem(p + panels - 1, panels) * 2 + q
    above = lax.rem(p + 1, panels) * 2 + q
    right = lax.rem(me + 1, spaces)
    left = lax.rem(me + spaces - 1, spaces)
    is_src = jnp.logical_and(p == last, q == 1)
    not_src = jnp.logical_or(p < last, q == 0)

    barrier = pltpu.get_barrier_semaphore()
    for other in (partner, below, above):
        pl.semaphore_signal(barrier, inc=1, device_id={"mode": other}, device_id_type=MESH)
    for d in range(1, spaces):
        pl.semaphore_signal(barrier, inc=1, device_id={"space": lax.rem(me + d, spaces)}, device_id_type=MESH)

    def chunk_of(m):
        c = m // (NPANEL * halves)
        h = lax.rem(m // NPANEL, halves)
        t = lax.rem(m, NPANEL)
        return c, t, h

    ext[:, cy : cy + cells] = modes_ref[...]

    @pl.when(is_src)
    def _():
        for a in range(pairs):
            advb[a] = modes_ref[:, 2 * a : 2 * a + 2]

    @pl.when(p == 0)
    def _():
        for m in range(chunks):
            c, h = m // (NPANEL * halves), (m // NPANEL) % halves
            up_in[m] = modes_ref[c, h * hc : (h + 1) * hc]

    @pl.when(p == last)
    def _():
        for m in range(chunks):
            c, h = m // (NPANEL * halves), (m // NPANEL) % halves
            dn_in[m] = modes_ref[c, h * hc : (h + 1) * hc]

    pl.semaphore_wait(barrier, 3 + spaces - 1)

    def copy_adv_down(a):
        return pltpu.make_async_remote_copy(
            src_ref=advb.at[q * quarter + a], dst_ref=advb.at[q * quarter + a],
            send_sem=ad_send.at[a], recv_sem=adv_recv.at[q * quarter + a],
            device_id={"mode": below}, device_id_type=MESH)

    def copy_adv_side(x):
        return pltpu.make_async_remote_copy(
            src_ref=advb.at[x], dst_ref=advb.at[x],
            send_sem=ay_send.at[x], recv_sem=adv_recv.at[x],
            device_id={"mode": partner}, device_id_type=MESH)

    def copy_up(m):
        return pltpu.make_async_remote_copy(
            src_ref=up_out.at[m], dst_ref=up_in.at[m], send_sem=up_send.at[m], recv_sem=up_recv.at[m],
            device_id={"mode": above}, device_id_type=MESH)

    def copy_down(m):
        return pltpu.make_async_remote_copy(
            src_ref=dn_out.at[m], dst_ref=dn_in.at[m], send_sem=dn_send.at[m], recv_sem=dn_recv.at[m],
            device_id={"mode": below}, device_id_type=MESH)

    def copy_side(m):
        return pltpu.make_async_remote_copy(
            src_ref=tests.at[m, q], dst_ref=tests.at[m, q], send_sem=y_send.at[m], recv_sem=y_recv.at[m],
            device_id={"mode": partner}, device_id_type=MESH)

    @pl.when(is_src)
    def _():
        for a in range(pairs):
            copy_adv_side(a).start()

    halo_up = pltpu.make_async_remote_copy(
        src_ref=modes_ref.at[:, pl.ds(cells - cy, cy)], dst_ref=ext.at[:, pl.ds(0, cy)],
        send_sem=halo_send.at[0], recv_sem=halo_recv.at[0], device_id={"space": right}, device_id_type=MESH)
    halo_down = pltpu.make_async_remote_copy(
        src_ref=modes_ref.at[:, pl.ds(0, cy)], dst_ref=ext.at[:, pl.ds(cells + cy, cy)],
        send_sem=halo_send.at[1], recv_sem=halo_recv.at[1], device_id={"space": left}, device_id_type=MESH)
    halo_up.start()
    halo_down.start()

    def values_of(xp):
        adv_at = advb.at[xp]
        for e in range(2):
            xy = 2 * xp + e
            x = xy // cy
            y = lax.rem(xy, cy)
            y_next = cy + x * cy + lax.rem(y + 1, cy)
            y_prev = cy + x * cy + lax.rem(y + cy - 1, cy)
            for d in range(3):
                advf[e, d] = adv_at[d, e].astype(F32)
            grads = []
            for c in range(comps):
                center = ext[c, xy + cy].astype(F32)
                gx = 0.5 * (ext[c, xy + 2 * cy].astype(F32) - ext[c, xy].astype(F32))
                gy = 0.5 * (ext[c, y_next].astype(F32) - ext[c, y_prev].astype(F32))
                gz = 0.5 * (pltpu.roll(center, lanes - 1, 1) - pltpu.roll(center, 1, 1))
                grads.append((gx, gy, gz))

            def row(j, carry):
                rows = [jnp.broadcast_to(advf[e, d, pl.ds(j, 1), :], (nm, lanes)) for d in range(3)]
                for c in range(comps):
                    value = rows[0] * grads[c][0] + rows[1] * grads[c][1] + rows[2] * grads[c][2]
                    start = pl.multiple_of(j * nm, nm)
                    vals[c * pairs + xp, pl.ds(start, nm), e * lanes : (e + 1) * lanes] = value.astype(BF16)
                return carry

            lax.fori_loop(0, nm, row, 0, unroll=4)

    def gemm(kb):
        c = kb // (pairs // 2)
        h = lax.rem(kb // (quarter // 2), halves)
        total = None
        for k in range(2):
            xp = lax.rem(kb, pairs // 2) * 2 + k
            for e in range(2):
                xy = 2 * xp + e
                xl = lax.rem(xy, hc)
                weight = weights_ref[pl.ds(xy, 1), :]
                for t in range(NPANEL):
                    for s in range(2):
                        raw = tests[(c * halves + h) * NPANEL + t, s, xl].astype(F32)
                        r = (t * 2 + s) * nm
                        wts[k, r : r + nm, e * lanes : (e + 1) * lanes] = (weight * raw).astype(BF16)
            part = lax.dot_general(vals[c * pairs + xp], wts[k], (((1,), (1,)), ((), ())), preferred_element_type=F32)
            total = part if total is None else total + part
        acc[...] += total

    off_up = SKEW * p
    off_adv = SKEW * (last - p)
    off_down = quarter + off_adv
    off_own = jnp.maximum(off_up, off_down)
    off_dot = off_own + 1 + SKEW
    ticks = quarter + SKEW * last + 1 + SKEW + chunks
    acc[...] = jnp.zeros_like(acc)

    def tick(step, carry):
        a = step - off_adv

        @pl.when(jnp.logical_and(a >= 0, a < quarter))
        def _():
            @pl.when(not_src)
            def _():
                copy_adv_side(q * quarter + a).wait_recv()

            @pl.when(p > 0)
            def _():
                copy_adv_down(a).start()

            @pl.when(p < last)
            def _():
                copy_adv_side(q * quarter + a).start()

        mu = step - off_up

        @pl.when(jnp.logical_and(mu >= 0, mu < chunks))
        def _():
            @pl.when(p > 0)
            def _():
                copy_up(mu).wait_recv()

            @pl.when(p < last)
            def _():
                c, t, h = chunk_of(mu)
                mine = modes_ref[c, pl.ds(h * hc, hc)]
                up_out[mu] = jnp.where(plan_ref[1 + t] == p, mine, up_in[mu])
                copy_up(mu).start()

        md = step - off_down

        @pl.when(jnp.logical_and(md >= 0, md < chunks))
        def _():
            @pl.when(p < last)
            def _():
                copy_down(md).wait_recv()

            @pl.when(p > 0)
            def _():
                c, t, h = chunk_of(md)
                mine = modes_ref[c, pl.ds(h * hc, hc)]
                dn_out[md] = jnp.where(plan_ref[1 + t] == p, mine, dn_in[md])
                copy_down(md).start()

        mf = step - off_own

        @pl.when(jnp.logical_and(mf >= 0, mf < chunks))
        def _():
            c, t, h = chunk_of(mf)
            mine = modes_ref[c, pl.ds(h * hc, hc)]
            owner = plan_ref[1 + t]
            got = jnp.where(owner < p, up_in[mf], dn_in[mf])
            tests[mf, q] = jnp.where(owner == p, mine, got)
            copy_side(mf).start()

        @pl.when(jnp.logical_and(a >= 0, a < pairs))
        def _():
            @pl.when(a == 0)
            def _():
                halo_up.wait_recv()
                halo_down.wait_recv()

            xp = lax.rem(q * quarter + a, pairs)

            @pl.when(jnp.logical_and(a >= quarter, not_src))
            def _():
                copy_adv_side(xp).wait_recv()

            values_of(xp)

        mg = step - off_dot

        @pl.when(jnp.logical_and(mg >= 0, mg < chunks))
        def _():
            @pl.when(lax.rem(mg, 2) == 0)
            def _():
                copy_side(mg).wait_recv()
                copy_side(mg + 1).wait_recv()

            gemm(mg)

        return carry

    lax.fori_loop(0, ticks, tick, 0)

    for jt in range(nm * nm // lanes):
        turned = acc[jt * lanes : (jt + 1) * lanes, :].T
        for s in range(spaces):
            piece = turned[s * own_rows : (s + 1) * own_rows]
            tot[s, :, jt * lanes : (jt + 1) * lanes] = piece
            stage[s, :, jt * lanes : (jt + 1) * lanes] = piece.astype(BF16)

    copies = []
    for d in range(1, spaces):
        peer = lax.rem(me + d, spaces)
        copies.append(pltpu.make_async_remote_copy(
            src_ref=stage.at[peer], dst_ref=rs_in.at[d - 1], send_sem=rs_send.at[d - 1],
            recv_sem=rs_recv.at[d - 1], device_id={"space": peer}, device_id_type=MESH))
    for copy in copies:
        copy.start()

    halo_up.wait_send()
    halo_down.wait_send()

    @pl.when(is_src)
    def _():
        for a in range(pairs):
            copy_adv_side(a).wait_send()

    @pl.when(p < last)
    def _():
        def done(a, carry):
            copy_adv_side(q * quarter + a).wait_send()
            return carry
        lax.fori_loop(0, quarter, done, 0)

        def done_up(m, carry):
            copy_up(m).wait_send()
            return carry
        lax.fori_loop(0, chunks, done_up, 0)

    @pl.when(p > 0)
    def _():
        def done(a, carry):
            copy_adv_down(a).wait_send()
            return carry
        lax.fori_loop(0, quarter, done, 0)

        def done_down(m, carry):
            copy_down(m).wait_send()
            return carry
        lax.fori_loop(0, chunks, done_down, 0)

    def done_side(m, carry):
        copy_side(m).wait_send()
        return carry

    lax.fori_loop(0, chunks, done_side, 0)

    total = tot[me]
    for d, copy in enumerate(copies):
        copy.wait_recv()
        total = total + rs_in[d].astype(F32)
    out_ref[...] = total
    for copy in copies:
        copy.wait_send()


def solution(mesh):
    nmode, spaces = mesh.shape["mode"], mesh.shape["space"]

    def local(modes, weights, plan):
        comps, nm, nx, cy, lanes = modes.shape
        cells = nx * cy
        assert PANEL == 2 * nm and nmode % 2 == 0
        test_count = NPANEL * PANEL
        own_rows = test_count // spaces
        turned = modes.transpose(0, 2, 3, 1, 4).reshape(comps, cells, nm, lanes)
        hc, pairs = cells // 2, cells // 2
        chunks = comps * NPANEL * 2
        quarter = pairs // 2
        vm = pl.BlockSpec(memory_space=pltpu.VMEM)
        chunk = (chunks, hc, nm, lanes)
        dma = pltpu.SemaphoreType.DMA
        out = pl.pallas_call(
            functools.partial(kernel, (nmode // 2, spaces, cy, own_rows)),
            out_shape=jax.ShapeDtypeStruct((own_rows, nm * nm), F32),
            in_specs=[pl.BlockSpec(memory_space=pltpu.SMEM), vm, vm],
            out_specs=vm,
            scratch_shapes=[
                pltpu.VMEM((comps, cells + 2 * cy, nm, lanes), BF16),
                pltpu.VMEM((pairs, comps, 2, nm, lanes), BF16),
                pltpu.VMEM(chunk, BF16), pltpu.VMEM(chunk, BF16), pltpu.VMEM(chunk, BF16), pltpu.VMEM(chunk, BF16),
                pltpu.VMEM((chunks, 2, hc, nm, lanes), BF16),
                pltpu.VMEM((2, comps, nm, lanes), F32),
                pltpu.VMEM((comps * pairs, nm * nm, 2 * lanes), BF16),
                pltpu.VMEM((2, test_count, 2 * lanes), BF16),
                pltpu.VMEM((nm * nm, test_count), F32),
                pltpu.VMEM((spaces, own_rows, nm * nm), F32),
                pltpu.VMEM((spaces, own_rows, nm * nm), BF16),
                pltpu.VMEM((spaces - 1, own_rows, nm * nm), BF16),
                dma((2,)), dma((2,)),
                dma((chunks,)), dma((chunks,)), dma((chunks,)), dma((chunks,)), dma((chunks,)), dma((chunks,)),
                dma((quarter,)), dma((pairs,)), dma((pairs,)),
                dma((spaces - 1,)), dma((spaces - 1,)),
            ],
            compiler_params=pltpu.CompilerParams(
                collective_id=0, has_side_effects=True, vmem_limit_bytes=48 * 1024 * 1024),
        )(plan, turned, weights.reshape(cells, lanes))
        return out.reshape(own_rows, nm, nm)

    in_specs = (P(None, "mode", "space", None, None), P("space", None, None), P())
    return jax.shard_map(local, mesh=mesh, in_specs=in_specs, out_specs=P("space", None, "mode"), check_vma=False)
```

```python
import functools

import jax
import jax.numpy as jnp
from jax import lax
from jax.experimental import pallas as pl
from jax.experimental.pallas import tpu as pltpu
from jax.sharding import PartitionSpec as P

PANEL = 64
NPANEL = 2
SKEW = 3
TAIL = 4
LEAD = 2
MESH = pl.DeviceIdType.MESH
F32 = jnp.float32
BF16 = jnp.bfloat16


def kernel(dims, plan_ref, modes_ref, weights_ref, out_ref,
           ext, advb, up_in, dn_in, up_out, dn_out, tests, advf, vals, wts, acc, tot, stage, rs_in,
           halo_send, halo_recv, up_send, up_recv, dn_send, dn_recv, y_send, y_recv,
           ad_send, ay_send, adv_recv, rs_send, rs_recv):
    panels, spaces, cy, own_rows = dims
    chunks, _, nm, lanes = modes_ref.shape
    nx = weights_ref.shape[0]
    comps, cells = chunks // nx, nx * cy
    pairs = cells // 2
    quarter = pairs // 2
    last = panels - 1
    mode = lax.axis_index("mode")
    p = mode // 2
    q = lax.rem(mode, 2)
    me = lax.axis_index("space")
    partner = p * 2 + (1 - q)
    below = lax.rem(p + panels - 1, panels) * 2 + q
    above = lax.rem(p + 1, panels) * 2 + q
    right = lax.rem(me + 1, spaces)
    left = lax.rem(me + spaces - 1, spaces)
    is_src = jnp.logical_and(p == last, q == 1)
    not_src = jnp.logical_or(p < last, q == 0)

    barrier = pltpu.get_barrier_semaphore()
    pl.semaphore_signal(barrier, inc=1, device_id={"mode": partner}, device_id_type=MESH)

    @pl.when(p > 0)
    def _():
        pl.semaphore_signal(barrier, inc=1, device_id={"mode": below}, device_id_type=MESH)

    @pl.when(p < last)
    def _():
        pl.semaphore_signal(barrier, inc=1, device_id={"mode": above}, device_id_type=MESH)

    for d in range(1, spaces):
        pl.semaphore_signal(barrier, inc=1, device_id={"space": lax.rem(me + d, spaces)}, device_id_type=MESH)

    for m in range(chunks):
        first = cy * (1 + m % nx)
        ext[m // nx, first : first + cy] = modes_ref[m]

    @pl.when(is_src)
    def _():
        for a in range(pairs):
            for c in range(comps):
                at = 2 * a % cy
                advb[a, c] = modes_ref[c * nx + 2 * a // cy, at : at + 2]

    @pl.when(p == 0)
    def _():
        for m in range(chunks):
            for t in range(NPANEL):
                up_in[m, t] = modes_ref[m]

    @pl.when(p == last)
    def _():
        for m in range(chunks):
            for t in range(NPANEL):
                dn_in[m, t] = modes_ref[m]

    pl.semaphore_wait(barrier, spaces + (p > 0).astype(jnp.int32) + (p < last).astype(jnp.int32))

    def copy_adv_down(a):
        return pltpu.make_async_remote_copy(
            src_ref=advb.at[q * quarter + a], dst_ref=advb.at[q * quarter + a],
            send_sem=ad_send.at[a], recv_sem=adv_recv.at[q * quarter + a],
            device_id={"mode": below}, device_id_type=MESH)

    def copy_adv_side(x):
        return pltpu.make_async_remote_copy(
            src_ref=advb.at[x], dst_ref=advb.at[x],
            send_sem=ay_send.at[x], recv_sem=adv_recv.at[x],
            device_id={"mode": partner}, device_id_type=MESH)

    def copy_up(m):
        return pltpu.make_async_remote_copy(
            src_ref=up_out.at[m], dst_ref=up_in.at[m], send_sem=up_send.at[m], recv_sem=up_recv.at[m],
            device_id={"mode": above}, device_id_type=MESH)

    def copy_down(m):
        return pltpu.make_async_remote_copy(
            src_ref=dn_out.at[m], dst_ref=dn_in.at[m], send_sem=dn_send.at[m], recv_sem=dn_recv.at[m],
            device_id={"mode": below}, device_id_type=MESH)

    def copy_side(m):
        return pltpu.make_async_remote_copy(
            src_ref=tests.at[m, q], dst_ref=tests.at[m, q], send_sem=y_send.at[m], recv_sem=y_recv.at[m],
            device_id={"mode": partner}, device_id_type=MESH)

    @pl.when(is_src)
    def _():
        for a in range(pairs):
            copy_adv_side(a).start()

    halos = []
    for c in range(comps):
        for k, (plane, at, peer) in enumerate(((nx - 1, 0, right), (0, cells + cy, left))):
            halos.append(pltpu.make_async_remote_copy(
                src_ref=modes_ref.at[c * nx + plane], dst_ref=ext.at[c, pl.ds(at, cy)],
                send_sem=halo_send.at[c, k], recv_sem=halo_recv.at[c, k],
                device_id={"space": peer}, device_id_type=MESH))
    for halo in halos:
        halo.start()

    def values_of(xp):
        adv_at = advb.at[xp]
        for e in range(2):
            xy = 2 * xp + e
            x = lax.div(xp, cy // 2)
            y = xy - x * cy
            y_next = cy + x * cy + lax.rem(y + 1, cy)
            y_prev = cy + x * cy + lax.rem(y + cy - 1, cy)
            for d in range(3):
                advf[e, d] = adv_at[d, e].astype(F32)
            grads = []
            for c in range(comps):
                center = ext[c, xy + cy].astype(F32)
                gx = 0.5 * (ext[c, xy + 2 * cy].astype(F32) - ext[c, xy].astype(F32))
                gy = 0.5 * (ext[c, y_next].astype(F32) - ext[c, y_prev].astype(F32))
                gz = 0.5 * (pltpu.roll(center, lanes - 1, 1) - pltpu.roll(center, 1, 1))
                grads.append((gx, gy, gz))

            def row(j, carry):
                rows = [jnp.broadcast_to(advf[e, d, pl.ds(j, 1), :], (nm, lanes)) for d in range(3)]
                for c in range(comps):
                    value = rows[0] * grads[c][0] + rows[1] * grads[c][1] + rows[2] * grads[c][2]
                    start = pl.multiple_of(j * nm, nm)
                    vals[c * pairs + xp, pl.ds(start, nm), e * lanes : (e + 1) * lanes] = value.astype(BF16)
                return carry

            lax.fori_loop(0, nm, row, 0, unroll=4)

    def gemm(m):
        plane = lax.rem(m, nx)
        total = None
        for k in range(cy // 2):
            for e in range(2):
                weight = weights_ref[plane, 2 * k + e : 2 * k + e + 1, :]
                for t in range(NPANEL):
                    for s in range(2):
                        raw = tests[m, s, t, 2 * k + e].astype(F32)
                        r = (t * 2 + s) * nm
                        wts[k, r : r + nm, e * lanes : (e + 1) * lanes] = (weight * raw).astype(BF16)
            part = lax.dot_general(vals[m * (cy // 2) + k], wts[k], (((1,), (1,)), ((), ())), preferred_element_type=F32)
            total = part if total is None else total + part
        acc[...] += total

    off_up = SKEW * p
    off_adv = SKEW * (last - p)
    off_down = quarter + off_adv
    off_own = jnp.maximum(off_up, off_down)
    off_dot = off_own + TAIL
    ticks = quarter + SKEW * last + TAIL + chunks
    acc[...] = jnp.zeros_like(acc)

    def tick(step, carry):
        a = step - off_adv - LEAD

        @pl.when(jnp.logical_and(a >= 0, a < quarter))
        def _():
            @pl.when(not_src)
            def _():
                copy_adv_side(q * quarter + a).wait_recv()

            @pl.when(p > 0)
            def _():
                copy_adv_down(a).start()

            @pl.when(p < last)
            def _():
                copy_adv_side(q * quarter + a).start()

        mu = step - off_up

        @pl.when(jnp.logical_and(mu >= 0, mu < chunks))
        def _():
            @pl.when(p > 0)
            def _():
                copy_up(mu).wait_recv()

            @pl.when(p < last)
            def _():
                mine = modes_ref[mu]
                for t in range(NPANEL):
                    up_out[mu, t] = jnp.where(plan_ref[1 + t] == p, mine, up_in[mu, t])
                copy_up(mu).start()

        early = step - off_adv
        md = jnp.where(early < LEAD, early, step - off_down)

        @pl.when(jnp.logical_and(md >= jnp.where(early < LEAD, 0, LEAD), md < chunks))
        def _():
            @pl.when(p < last)
            def _():
                copy_down(md).wait_recv()

            @pl.when(p > 0)
            def _():
                mine = modes_ref[md]
                for t in range(NPANEL):
                    dn_out[md, t] = jnp.where(plan_ref[1 + t] == p, mine, dn_in[md, t])
                copy_down(md).start()

        mf = step - off_own

        @pl.when(jnp.logical_and(mf >= 0, mf < chunks))
        def _():
            mine = modes_ref[mf]
            for t in range(NPANEL):
                owner = plan_ref[1 + t]
                got = jnp.where(owner < p, up_in[mf, t], dn_in[mf, t])
                tests[mf, q, t] = jnp.where(owner == p, mine, got)
            copy_side(mf).start()

        @pl.when(jnp.logical_and(a >= 0, a < pairs))
        def _():
            @pl.when(a == 0)
            def _():
                for halo in halos:
                    halo.wait_recv()

            xp = lax.rem(q * quarter + a, pairs)

            @pl.when(jnp.logical_and(a >= quarter, not_src))
            def _():
                copy_adv_side(xp).wait_recv()

            values_of(xp)

        mg = step - off_dot

        @pl.when(jnp.logical_and(mg >= 0, mg < chunks))
        def _():
            copy_side(mg).wait_recv()
            gemm(mg)

        return carry

    lax.fori_loop(0, ticks, tick, 0)

    for jt in range(nm * nm // lanes):
        turned = acc[jt * lanes : (jt + 1) * lanes, :].T
        for s in range(spaces):
            piece = turned[s * own_rows : (s + 1) * own_rows]
            tot[s, :, jt * lanes : (jt + 1) * lanes] = piece
            stage[s, :, jt * lanes : (jt + 1) * lanes] = piece.astype(BF16)

    copies = []
    for d in range(1, spaces):
        peer = lax.rem(me + d, spaces)
        copies.append(pltpu.make_async_remote_copy(
            src_ref=stage.at[peer], dst_ref=rs_in.at[d - 1], send_sem=rs_send.at[d - 1],
            recv_sem=rs_recv.at[d - 1], device_id={"space": peer}, device_id_type=MESH))
    for copy in copies:
        copy.start()

    for halo in halos:
        halo.wait_send()

    @pl.when(is_src)
    def _():
        for a in range(pairs):
            copy_adv_side(a).wait_send()

    @pl.when(p < last)
    def _():
        def done(a, carry):
            copy_adv_side(q * quarter + a).wait_send()
            return carry
        lax.fori_loop(0, quarter, done, 0)

        def done_up(m, carry):
            copy_up(m).wait_send()
            return carry
        lax.fori_loop(0, chunks, done_up, 0)

    @pl.when(p > 0)
    def _():
        def done(a, carry):
            copy_adv_down(a).wait_send()
            return carry
        lax.fori_loop(0, quarter, done, 0)

        def done_down(m, carry):
            copy_down(m).wait_send()
            return carry
        lax.fori_loop(0, chunks, done_down, 0)

    def done_side(m, carry):
        copy_side(m).wait_send()
        return carry

    lax.fori_loop(0, chunks, done_side, 0)

    total = tot[me]
    for d, copy in enumerate(copies):
        copy.wait_recv()
        total = total + rs_in[d].astype(F32)
    out_ref[...] = total
    for copy in copies:
        copy.wait_send()


def solution(mesh):
    nmode, spaces = mesh.shape["mode"], mesh.shape["space"]

    def local(modes, weights, plan):
        comps, nm, nx, cy, lanes = modes.shape
        cells = nx * cy
        assert PANEL == 2 * nm and nmode % 2 == 0
        test_count = NPANEL * PANEL
        own_rows = test_count // spaces
        turned = modes.transpose(0, 2, 3, 1, 4).reshape(comps * nx, cy, nm, lanes)
        pairs = cells // 2
        chunks = comps * nx
        quarter = pairs // 2
        vm = pl.BlockSpec(memory_space=pltpu.VMEM)
        chunk = (chunks, NPANEL, cy, nm, lanes)
        dma = pltpu.SemaphoreType.DMA
        out = pl.pallas_call(
            functools.partial(kernel, (nmode // 2, spaces, cy, own_rows)),
            out_shape=jax.ShapeDtypeStruct((own_rows, nm * nm), F32),
            in_specs=[pl.BlockSpec(memory_space=pltpu.SMEM), vm, vm],
            out_specs=vm,
            scratch_shapes=[
                pltpu.VMEM((comps, cells + 2 * cy, nm, lanes), BF16),
                pltpu.VMEM((pairs, comps, 2, nm, lanes), BF16),
                pltpu.VMEM(chunk, BF16), pltpu.VMEM(chunk, BF16), pltpu.VMEM(chunk, BF16), pltpu.VMEM(chunk, BF16),
                pltpu.VMEM((chunks, 2, NPANEL, cy, nm, lanes), BF16),
                pltpu.VMEM((2, comps, nm, lanes), F32),
                pltpu.VMEM((comps * pairs, nm * nm, 2 * lanes), BF16),
                pltpu.VMEM((cy // 2, test_count, 2 * lanes), BF16),
                pltpu.VMEM((nm * nm, test_count), F32),
                pltpu.VMEM((spaces, own_rows, nm * nm), F32),
                pltpu.VMEM((spaces, own_rows, nm * nm), BF16),
                pltpu.VMEM((spaces - 1, own_rows, nm * nm), BF16),
                dma((comps, 2)), dma((comps, 2)),
                dma((chunks,)), dma((chunks,)), dma((chunks,)), dma((chunks,)), dma((chunks,)), dma((chunks,)),
                dma((quarter,)), dma((pairs,)), dma((pairs,)),
                dma((spaces - 1,)), dma((spaces - 1,)),
            ],
            compiler_params=pltpu.CompilerParams(
                collective_id=0, has_side_effects=True, vmem_limit_bytes=48 * 1024 * 1024),
        )(plan, turned, weights)
        return out.reshape(own_rows, nm, nm)

    in_specs = (P(None, "mode", "space", None, None), P("space", None, None), P())
    return jax.shard_map(local, mesh=mesh, in_specs=in_specs, out_specs=P("space", None, "mode"), check_vma=False)
```

```python
import functools

import jax
import jax.numpy as jnp
from jax import lax
from jax.experimental import pallas as pl
from jax.experimental.pallas import tpu as pltpu
from jax.sharding import PartitionSpec as P

PANEL = 64
NPANEL = 2
SKEW = 3
TAIL = 4
LEAD = 2
MESH = pl.DeviceIdType.MESH
F32 = jnp.float32
BF16 = jnp.bfloat16


def kernel(dims, plan_ref, modes_ref, weights_ref, out_ref,
           ext, advb, up_in, dn_in, up_out, dn_out, tests, advf, vals, wts, acc, tot, stage, rs_in,
           halo_send, halo_recv, up_send, up_recv, dn_send, dn_recv, y_send, y_recv,
           ad_send, ay_send, adv_recv, rs_send, rs_recv):
    panels, spaces, cy, own_rows = dims
    chunks, _, nm, lanes = modes_ref.shape
    nx = weights_ref.shape[0]
    comps, cells = chunks // nx, nx * cy
    pairs = cells // 2
    quarter = pairs // 2
    last = panels - 1
    mode = lax.axis_index("mode")
    p = mode // 2
    q = lax.rem(mode, 2)
    me = lax.axis_index("space")
    partner = p * 2 + (1 - q)
    below = lax.rem(p + panels - 1, panels) * 2 + q
    above = lax.rem(p + 1, panels) * 2 + q
    right = lax.rem(me + 1, spaces)
    left = lax.rem(me + spaces - 1, spaces)
    is_src = jnp.logical_and(p == last, q == 1)
    not_src = jnp.logical_or(p < last, q == 0)

    barrier = pltpu.get_barrier_semaphore()
    pl.semaphore_signal(barrier, inc=1, device_id={"mode": partner}, device_id_type=MESH)

    @pl.when(p > 0)
    def _():
        pl.semaphore_signal(barrier, inc=1, device_id={"mode": below}, device_id_type=MESH)

    @pl.when(p < last)
    def _():
        pl.semaphore_signal(barrier, inc=1, device_id={"mode": above}, device_id_type=MESH)

    for d in range(1, spaces):
        pl.semaphore_signal(barrier, inc=1, device_id={"space": lax.rem(me + d, spaces)}, device_id_type=MESH)

    for m in range(chunks):
        first = cy * (1 + m % nx)
        ext[m // nx, first : first + cy] = modes_ref[m]

    @pl.when(is_src)
    def _():
        for a in range(pairs):
            for c in range(comps):
                at = 2 * a % cy
                advb[a, c] = modes_ref[c * nx + 2 * a // cy, at : at + 2]

    @pl.when(p == 0)
    def _():
        for m in range(chunks):
            for t in range(NPANEL):
                up_in[m, t] = modes_ref[m]

    @pl.when(p == last)
    def _():
        for m in range(chunks):
            for t in range(NPANEL):
                dn_in[m, t] = modes_ref[m]

    pl.semaphore_wait(barrier, spaces + (p > 0).astype(jnp.int32) + (p < last).astype(jnp.int32))

    def copy_adv_down(a):
        return pltpu.make_async_remote_copy(
            src_ref=advb.at[q * quarter + a], dst_ref=advb.at[q * quarter + a],
            send_sem=ad_send.at[a], recv_sem=adv_recv.at[q * quarter + a],
            device_id={"mode": below}, device_id_type=MESH)

    def copy_adv_side(x):
        return pltpu.make_async_remote_copy(
            src_ref=advb.at[x], dst_ref=advb.at[x],
            send_sem=ay_send.at[x], recv_sem=adv_recv.at[x],
            device_id={"mode": partner}, device_id_type=MESH)

    def copy_up(m, t):
        return pltpu.make_async_remote_copy(
            src_ref=up_out.at[m, t], dst_ref=up_in.at[m, t], send_sem=up_send.at[m, t], recv_sem=up_recv.at[m, t],
            device_id={"mode": above}, device_id_type=MESH)

    def copy_down(m, t):
        return pltpu.make_async_remote_copy(
            src_ref=dn_out.at[m, t], dst_ref=dn_in.at[m, t], send_sem=dn_send.at[m, t], recv_sem=dn_recv.at[m, t],
            device_id={"mode": below}, device_id_type=MESH)

    def copy_side(m):
        return pltpu.make_async_remote_copy(
            src_ref=tests.at[m, q], dst_ref=tests.at[m, q], send_sem=y_send.at[m], recv_sem=y_recv.at[m],
            device_id={"mode": partner}, device_id_type=MESH)

    @pl.when(is_src)
    def _():
        for a in range(pairs):
            copy_adv_side(a).start()

    halos = []
    for c in range(comps):
        for k, (plane, at, peer) in enumerate(((nx - 1, 0, right), (0, cells + cy, left))):
            halos.append(pltpu.make_async_remote_copy(
                src_ref=modes_ref.at[c * nx + plane], dst_ref=ext.at[c, pl.ds(at, cy)],
                send_sem=halo_send.at[c, k], recv_sem=halo_recv.at[c, k],
                device_id={"space": peer}, device_id_type=MESH))
    for halo in halos:
        halo.start()

    def values_of(xp):
        adv_at = advb.at[xp]
        for e in range(2):
            xy = 2 * xp + e
            x = lax.div(xp, cy // 2)
            y = xy - x * cy
            y_next = cy + x * cy + lax.rem(y + 1, cy)
            y_prev = cy + x * cy + lax.rem(y + cy - 1, cy)
            for d in range(3):
                advf[e, d] = adv_at[d, e].astype(F32)
            grads = []
            for c in range(comps):
                center = ext[c, xy + cy].astype(F32)
                gx = 0.5 * (ext[c, xy + 2 * cy].astype(F32) - ext[c, xy].astype(F32))
                gy = 0.5 * (ext[c, y_next].astype(F32) - ext[c, y_prev].astype(F32))
                gz = 0.5 * (pltpu.roll(center, lanes - 1, 1) - pltpu.roll(center, 1, 1))
                grads.append((gx, gy, gz))

            def row(j, carry):
                rows = [jnp.broadcast_to(advf[e, d, pl.ds(j, 1), :], (nm, lanes)) for d in range(3)]
                for c in range(comps):
                    value = rows[0] * grads[c][0] + rows[1] * grads[c][1] + rows[2] * grads[c][2]
                    start = pl.multiple_of(j * nm, nm)
                    vals[c * pairs + xp, pl.ds(start, nm), e * lanes : (e + 1) * lanes] = value.astype(BF16)
                return carry

            lax.fori_loop(0, nm, row, 0, unroll=4)

    def gemm(m):
        plane = lax.rem(m, nx)
        total = None
        for k in range(cy // 2):
            for e in range(2):
                weight = weights_ref[plane, 2 * k + e : 2 * k + e + 1, :]
                for t in range(NPANEL):
                    for s in range(2):
                        raw = tests[m, s, t, 2 * k + e].astype(F32)
                        r = (t * 2 + s) * nm
                        wts[k, r : r + nm, e * lanes : (e + 1) * lanes] = (weight * raw).astype(BF16)
            part = lax.dot_general(vals[m * (cy // 2) + k], wts[k], (((1,), (1,)), ((), ())), preferred_element_type=F32)
            total = part if total is None else total + part
        acc[...] += total

    off_up = SKEW * p
    off_adv = SKEW * (last - p)
    off_down = quarter + off_adv
    off_own = jnp.maximum(off_up, off_down)
    off_dot = off_own + TAIL
    ticks = quarter + SKEW * last + TAIL + chunks
    acc[...] = jnp.zeros_like(acc)

    def tick(step, carry):
        a = step - off_adv - LEAD

        @pl.when(jnp.logical_and(a >= 0, a < quarter))
        def _():
            @pl.when(not_src)
            def _():
                copy_adv_side(q * quarter + a).wait_recv()

            @pl.when(p > 0)
            def _():
                copy_adv_down(a).start()

            @pl.when(p < last)
            def _():
                copy_adv_side(q * quarter + a).start()

        mu = step - off_up

        @pl.when(jnp.logical_and(mu >= 0, mu < chunks))
        def _():
            for t in range(NPANEL):
                @pl.when(p > 0)
                def _():
                    copy_up(mu, t).wait_recv()

                @pl.when(p < last)
                def _():
                    up_out[mu, t] = jnp.where(plan_ref[1 + t] == p, modes_ref[mu], up_in[mu, t])
                    copy_up(mu, t).start()

        early = step - off_adv
        md = jnp.where(early < LEAD, early, step - off_down)

        @pl.when(jnp.logical_and(md >= jnp.where(early < LEAD, 0, LEAD), md < chunks))
        def _():
            for t in range(NPANEL):
                @pl.when(p < last)
                def _():
                    copy_down(md, t).wait_recv()

                @pl.when(p > 0)
                def _():
                    dn_out[md, t] = jnp.where(plan_ref[1 + t] == p, modes_ref[md], dn_in[md, t])
                    copy_down(md, t).start()

        mf = step - off_own

        @pl.when(jnp.logical_and(mf >= 0, mf < chunks))
        def _():
            mine = modes_ref[mf]
            for t in range(NPANEL):
                owner = plan_ref[1 + t]
                got = jnp.where(owner < p, up_in[mf, t], dn_in[mf, t])
                tests[mf, q, t] = jnp.where(owner == p, mine, got)
            copy_side(mf).start()

        @pl.when(jnp.logical_and(a >= 0, a < pairs))
        def _():
            @pl.when(a == 0)
            def _():
                for halo in halos:
                    halo.wait_recv()

            xp = lax.rem(q * quarter + a, pairs)

            @pl.when(jnp.logical_and(a >= quarter, not_src))
            def _():
                copy_adv_side(xp).wait_recv()

            values_of(xp)

        mg = step - off_dot

        @pl.when(jnp.logical_and(mg >= 0, mg < chunks))
        def _():
            copy_side(mg).wait_recv()
            gemm(mg)

        return carry

    lax.fori_loop(0, ticks, tick, 0)

    for jt in range(nm * nm // lanes):
        turned = acc[jt * lanes : (jt + 1) * lanes, :].T
        for s in range(spaces):
            piece = turned[s * own_rows : (s + 1) * own_rows]
            tot[s, :, jt * lanes : (jt + 1) * lanes] = piece
            stage[s, :, jt * lanes : (jt + 1) * lanes] = piece.astype(BF16)

    copies = []
    for d in range(1, spaces):
        peer = lax.rem(me + d, spaces)
        copies.append(pltpu.make_async_remote_copy(
            src_ref=stage.at[peer], dst_ref=rs_in.at[d - 1], send_sem=rs_send.at[d - 1],
            recv_sem=rs_recv.at[d - 1], device_id={"space": peer}, device_id_type=MESH))
    for copy in copies:
        copy.start()

    for halo in halos:
        halo.wait_send()

    @pl.when(is_src)
    def _():
        for a in range(pairs):
            copy_adv_side(a).wait_send()

    @pl.when(p < last)
    def _():
        def done(a, carry):
            copy_adv_side(q * quarter + a).wait_send()
            return carry
        lax.fori_loop(0, quarter, done, 0)

        def done_up(m, carry):
            for t in range(NPANEL):
                copy_up(m, t).wait_send()
            return carry
        lax.fori_loop(0, chunks, done_up, 0)

    @pl.when(p > 0)
    def _():
        def done(a, carry):
            copy_adv_down(a).wait_send()
            return carry
        lax.fori_loop(0, quarter, done, 0)

        def done_down(m, carry):
            for t in range(NPANEL):
                copy_down(m, t).wait_send()
            return carry
        lax.fori_loop(0, chunks, done_down, 0)

    def done_side(m, carry):
        copy_side(m).wait_send()
        return carry

    lax.fori_loop(0, chunks, done_side, 0)

    total = tot[me]
    for d, copy in enumerate(copies):
        copy.wait_recv()
        total = total + rs_in[d].astype(F32)
    out_ref[...] = total
    for copy in copies:
        copy.wait_send()


def solution(mesh):
    nmode, spaces = mesh.shape["mode"], mesh.shape["space"]

    def local(modes, weights, plan):
        comps, nm, nx, cy, lanes = modes.shape
        cells = nx * cy
        assert PANEL == 2 * nm and nmode % 2 == 0
        test_count = NPANEL * PANEL
        own_rows = test_count // spaces
        turned = modes.transpose(0, 2, 3, 1, 4).reshape(comps * nx, cy, nm, lanes)
        pairs = cells // 2
        chunks = comps * nx
        quarter = pairs // 2
        vm = pl.BlockSpec(memory_space=pltpu.VMEM)
        chunk = (chunks, NPANEL, cy, nm, lanes)
        dma = pltpu.SemaphoreType.DMA
        out = pl.pallas_call(
            functools.partial(kernel, (nmode // 2, spaces, cy, own_rows)),
            out_shape=jax.ShapeDtypeStruct((own_rows, nm * nm), F32),
            in_specs=[pl.BlockSpec(memory_space=pltpu.SMEM), vm, vm],
            out_specs=vm,
            scratch_shapes=[
                pltpu.VMEM((comps, cells + 2 * cy, nm, lanes), BF16),
                pltpu.VMEM((pairs, comps, 2, nm, lanes), BF16),
                pltpu.VMEM(chunk, BF16), pltpu.VMEM(chunk, BF16), pltpu.VMEM(chunk, BF16), pltpu.VMEM(chunk, BF16),
                pltpu.VMEM((chunks, 2, NPANEL, cy, nm, lanes), BF16),
                pltpu.VMEM((2, comps, nm, lanes), F32),
                pltpu.VMEM((comps * pairs, nm * nm, 2 * lanes), BF16),
                pltpu.VMEM((cy // 2, test_count, 2 * lanes), BF16),
                pltpu.VMEM((nm * nm, test_count), F32),
                pltpu.VMEM((spaces, own_rows, nm * nm), F32),
                pltpu.VMEM((spaces, own_rows, nm * nm), BF16),
                pltpu.VMEM((spaces - 1, own_rows, nm * nm), BF16),
                dma((comps, 2)), dma((comps, 2)),
                *[dma((chunks, NPANEL))] * 4, dma((chunks,)), dma((chunks,)),
                dma((quarter,)), dma((pairs,)), dma((pairs,)),
                dma((spaces - 1,)), dma((spaces - 1,)),
            ],
            compiler_params=pltpu.CompilerParams(
                collective_id=0, has_side_effects=True, vmem_limit_bytes=48 * 1024 * 1024),
        )(plan, turned, weights)
        return out.reshape(own_rows, nm, nm)

    in_specs = (P(None, "mode", "space", None, None), P("space", None, None), P())
    return jax.shard_map(local, mesh=mesh, in_specs=in_specs, out_specs=P("space", None, "mode"), check_vma=False)
```
